256 devices in a mesh: dp: 4 (over x), pipe: 4 (over z_hi, core), tensor: 16 (over y, z_lo).
Axes of the slice: x: 4, y: 4, z: 8 (z_hi: 2, z_lo: 4; z = z_hi * 4 + z_lo), core: 2. Of those that a mesh axis runs over, the one named last changes fastest.
Arguments:
- inputs: bfloat16 [4, 896, 8192], P('pipe', 'dp', 'tensor'), may hold values from -6 to 6
- cotangent: bfloat16 [896, 8192], P('dp', 'tensor'), may hold values from -6 to 6
- up_first: bfloat16 [4, 32, 256, 256], P('pipe', 'tensor'), may hold values from -0.375 to 0.375
- up_second: bfloat16 [4, 32, 256, 1024], P('pipe', 'tensor'), may hold values from -0.375 to 0.375
- down_first: bfloat16 [4, 32, 1024, 256], P('pipe', 'tensor'), may hold values from -0.1875 to 0.1875
- down_second: bfloat16 [4, 32, 256, 256], P('pipe', 'tensor'), may hold values from -0.375 to 0.375
Outputs:
- grad_inputs: bfloat16 [4, 896, 8192], P('pipe', 'dp', 'tensor')
- grad_up_first: float32 [4, 32, 256, 256], P('pipe', 'tensor', 'dp')
- grad_up_second: float32 [4, 32, 256, 1024], P('pipe', 'tensor', 'dp')
- grad_down_first: float32 [4, 32, 1024, 256], P('pipe', 'tensor', 'dp')
- grad_down_second: float32 [4, 32, 256, 256], P('pipe', 'tensor', 'dp')
The draws below stay inside these ranges and needn't reach their ends.
All inputs are finite; a program needn't handle non-finite values.
Results may differ from the reference program's by a relative error of at most 0.018.
Values may be sent and summed in bfloat16 or wider, within the bound.
No kernel may reach another device: no remote copies, remote signals or barrier semaphores. Data moves between devices by JAX's collectives and lax.ppermute only.
A program may use at most 64 MiB of HBM per device.

```python
import math
import jax
import jax.numpy as jnp

NB = 32
BS = 256
HB = 1024
D = 8192
LAYERS = 4
TOKENS = 896


def level_of(key, dims, shards, smallest, largest):
    gain = 1.0
    for axis_at, parts in shards:
        steps = jax.random.uniform(jax.random.fold_in(jax.random.fold_in(key, 6), axis_at), (parts,), jnp.float32, smallest / len(shards), largest / len(shards))
        gain = gain * jnp.repeat(jnp.exp(steps), dims[axis_at] // parts).reshape((-1,) + (1,) * (len(dims) - 1 - axis_at))
    return gain


def noise(own_key, dims, deviation, limit, cuts=(), kind=jnp.bfloat16):
    values = jax.random.normal(own_key, dims, jnp.float32) * deviation
    if len(cuts) > 0:
        values = level_of(own_key, dims, cuts, -0.22, 0.18) * values
    return jnp.clip(values, min=-limit, max=limit).astype(kind)


def setup_inputs(seed: int = 0) -> dict:
    splits = jax.random.split(jax.random.key(seed), 7)
    return {
        "inputs": noise(splits[0], (LAYERS, TOKENS, D), 1.0, 6.0, ((0, 4), (1, 4), (2, 16))),
        "cotangent": noise(splits[1], (TOKENS, D), 1.0, 6.0, ((0, 4), (1, 16))),
        "up_first": noise(splits[2], (LAYERS, NB, BS, BS), BS ** -0.5, 0.375, ((0, 4), (1, 16))),
        "up_second": noise(splits[3], (LAYERS, NB, BS, HB), BS ** -0.5, 0.375, ((0, 4), (1, 16))),
        "down_first": noise(splits[4], (LAYERS, NB, HB, BS), HB ** -0.5, 0.1875, ((0, 4), (1, 16))),
        "down_second": noise(splits[5], (LAYERS, NB, BS, BS), BS ** -0.5, 0.375, ((0, 4), (1, 16))),
    }


root_half = 1.0 / math.sqrt(2.0)
norm_density = 1.0 / math.sqrt(2.0 * math.pi)

def gelu_value(values):
    return values * 0.5 * (1.0 + jax.scipy.special.erf(values * root_half))

def gelu_slope(values):
    cumulative = 0.5 * (1.0 + jax.scipy.special.erf(values * root_half))
    return cumulative + values * jnp.exp(-0.5 * values * values) * norm_density

def permute(matrix):
    row_count = matrix.shape[0]
    shaped = matrix.reshape(row_count, NB, NB, BS // NB).transpose(0, 2, 1, 3)
    return shaped.reshape(row_count, NB * BS)

def block_apply(matrix, weight):
    row_count = matrix.shape[0]
    shaped = matrix.astype(jnp.float32).reshape(row_count, NB, -1)
    result = jnp.einsum('tic,ice->tie', shaped, weight.astype(jnp.float32))
    return result.reshape(row_count, -1)

def block_apply_back(matrix, weight):
    row_count = matrix.shape[0]
    shaped = matrix.astype(jnp.float32).reshape(row_count, NB, -1)
    result = jnp.einsum('tie,ice->tic', shaped, weight.astype(jnp.float32))
    return result.reshape(row_count, -1)

def weight_grad(left, right, factor):
    row_count = left.shape[0]
    left_blocks = left.astype(jnp.float32).reshape(row_count, NB, -1)
    right_blocks = right.astype(jnp.float32).reshape(row_count, NB, -1)
    return jnp.einsum('tic,tie->ice', left_blocks, right_blocks) * factor

def reference(inputs, cotangent, up_first, up_second, down_first, down_second):
    factor = 1.0 / math.sqrt(TOKENS)
    incoming = cotangent
    grads_x, grads_a, grads_b, grads_c, grads_d = ([], [], [], [], [])
    for layer in range(LAYERS - 1, -1, -1):
        acts = inputs[layer]
        first = block_apply(acts, up_first[layer]).astype(jnp.bfloat16)
        mixed = permute(first)
        pre = block_apply(mixed, up_second[layer])
        hidden = gelu_value(pre).astype(jnp.bfloat16)
        down = block_apply(hidden, down_first[layer]).astype(jnp.bfloat16)
        last = permute(down)
        grad_last = block_apply_back(incoming, down_second[layer]).astype(jnp.bfloat16)
        grad_down = permute(grad_last)
        grad_hidden = block_apply_back(grad_down, down_first[layer])
        grad_pre = (grad_hidden * gelu_slope(pre)).astype(jnp.bfloat16)
        grad_mixed = block_apply_back(grad_pre, up_second[layer]).astype(jnp.bfloat16)
        grad_first = permute(grad_mixed)
        grad_acts = (incoming.astype(jnp.float32) + block_apply_back(grad_first, up_first[layer])).astype(jnp.bfloat16)
        grads_x.append(grad_acts)
        grads_a.append(weight_grad(acts, grad_first, factor))
        grads_b.append(weight_grad(mixed, grad_pre, factor))
        grads_c.append(weight_grad(hidden, grad_down, factor))
        grads_d.append(weight_grad(last, incoming, factor))
        incoming = grad_acts
    return (jnp.stack(grads_x[::-1]), jnp.stack(grads_a[::-1]), jnp.stack(grads_b[::-1]), jnp.stack(grads_c[::-1]), jnp.stack(grads_d[::-1]))
```

```python
import functools
import math

import jax
import jax.numpy as jnp
from jax import lax
from jax.experimental import pallas as pl
from jax.experimental.pallas import tpu as pltpu
from jax.sharding import PartitionSpec as P

root_half = 1.0 / math.sqrt(2.0)
norm_density = 1.0 / math.sqrt(2.0 * math.pi)
f32 = jnp.float32
bf16 = jnp.bfloat16


def dot(a, b, dims):
    return lax.dot_general(a, b, (dims, ((), ())), preferred_element_type=f32)


def nn(a, b):
    return dot(a, b, ((1,), (0,)))


def nt(a, b):
    return dot(a, b, ((1,), (1,)))


def pack(out_ref, at, parts, peers):
    tokens = parts[0].shape[1]
    shaped = [part.reshape(peers, 2, 8, tokens) for part in parts]
    joined = jnp.stack(shaped, axis=2).reshape(peers, 2, 16, tokens).astype(bf16)
    out_ref[:, at : at + 2] = joined


def unpack(ref, at):
    peers, _, rows, tokens = ref.shape
    return ref[:, at].reshape(peers * rows, tokens)


def call(body, outs, args, flops=0, scalars=0):
    moved = sum(a.size * a.dtype.itemsize for a in args) + sum(
        o.size * o.dtype.itemsize for o in outs
    )
    specs = [pl.BlockSpec(memory_space=pltpu.SMEM)] * scalars
    specs += [pl.BlockSpec(memory_space=pltpu.VMEM)] * (len(args) - scalars)
    return pl.pallas_call(
        body,
        out_shape=outs,
        in_specs=specs,
        out_specs=[pl.BlockSpec(memory_space=pltpu.VMEM)] * len(outs),
        cost_estimate=pl.CostEstimate(flops=flops, bytes_accessed=moved, transcendentals=0),
    )(*args)


def struct(shape, dtype=bf16):
    return jax.ShapeDtypeStruct(shape, dtype)


def entry_kernel(x_ref, g_ref, u1_ref, d2_ref, out_ref):
    peers = out_ref.shape[0]
    width = u1_ref.shape[1]
    firsts, lasts = [], []
    for i in range(2):
        cols = slice(i * width, (i + 1) * width)
        firsts.append(nn(x_ref[:, cols], u1_ref[i]).T)
        lasts.append(nt(d2_ref[i], g_ref[:, cols]))
    pack(out_ref, 0, firsts, peers)
    pack(out_ref, 2, lasts, peers)


def turn_kernel(x_ref, g_ref, xt_ref, gt_ref):
    width = xt_ref.shape[1]
    for i in range(2):
        cols = slice(i * width, (i + 1) * width)
        xt_ref[i] = x_ref[:, cols].astype(f32).T.astype(bf16)
        gt_ref[i] = g_ref[:, cols].astype(f32).T.astype(bf16)


def flip_kernel(u2_ref, d1_ref, u2t_ref, d1t_ref):
    for j in range(2):
        u2t_ref[j] = u2_ref[j].astype(f32).T.astype(bf16)
        d1t_ref[j] = d1_ref[j].astype(f32).T.astype(bf16)


def forward_kernel(
    last_ref, r_ref, u2t_ref, d1t_ref, d1_ref, u2_ref, out_ref, slope_ref, hid_ref, gp_ref
):
    peers = out_ref.shape[0]
    hidden = u2t_ref.shape[1]
    step = 256
    for j in range(2):
        mixed = unpack(r_ref, j)
        for h in range(0, hidden, step):
            pre = nn(u2t_ref[j, h : h + step], mixed)
            cumulative = 0.5 * (1.0 + lax.erf(pre * root_half))
            hid_ref[j, h : h + step] = (pre * cumulative).astype(bf16)
            slope_ref[j, h : h + step] = (
                cumulative + pre * jnp.exp(-0.5 * pre * pre) * norm_density
            )

    @pl.when(last_ref[0] == 1)
    def _():
        backward(r_ref, 2, slope_ref, d1_ref, u2_ref, out_ref, gp_ref)

    @pl.when(last_ref[0] == 0)
    def _():
        pack(out_ref, 0, [nn(d1t_ref[j], hid_ref[j]) for j in range(2)], peers)


def backward(r_ref, at, slope_ref, d1_ref, u2_ref, out_ref, gp_ref):
    hidden = d1_ref.shape[1]
    step = 256
    mixes = []
    for j in range(2):
        grad_down = unpack(r_ref, at + j)
        for h in range(0, hidden, step):
            grad_hidden = nn(d1_ref[j, h : h + step], grad_down)
            gp_ref[j, h : h + step] = (grad_hidden * slope_ref[j, h : h + step]).astype(bf16)
        mixes.append(nn(u2_ref[j], gp_ref[j]))
    pack(out_ref, 0, mixes, out_ref.shape[0])


def middle_kernel(r_ref, slope_ref, d1_ref, u2_ref, out_ref, gp_ref):
    backward(r_ref, 0, slope_ref, d1_ref, u2_ref, out_ref, gp_ref)


def down_kernel(hid_ref, d1t_ref, out_ref):
    pack(out_ref, 0, [nn(d1t_ref[j], hid_ref[j]) for j in range(2)], out_ref.shape[0])


def head_kernel(gt_ref, d2_ref, out_ref):
    pack(out_ref, 0, [nn(d2_ref[i], gt_ref[i]) for i in range(2)], out_ref.shape[0])


def tail_kernel(r_ref, gt_ref, u1_ref, out_ref):
    for i in range(2):
        acts = nn(u1_ref[i], unpack(r_ref, i))
        out_ref[i] = (gt_ref[i].astype(f32) + acts).astype(bf16)


def rows_kernel(gt_ref, out_ref):
    width = gt_ref.shape[1]
    for i in range(2):
        out_ref[:, i * width : (i + 1) * width] = gt_ref[i].astype(f32).T.astype(bf16)


def main_terms_kernel(dp_ref, last_ref, gt_ref, hid_ref, gd_ref, mixed_ref, gp_ref, *outs, at):
    shares = len(outs)
    width = gt_ref.shape[1]
    hidden = hid_ref.shape[1]
    tokens = gt_ref.shape[2]
    part, deep = width // shares, hidden // shares
    tiles = part // 16
    for j in range(2):
        g = gt_ref[j]
        grad_down = unpack(gd_ref, at + j)
        for k in range(shares):
            d = lax.rem(dp_ref[0] + k, shares)
            out = outs[k]
            low = last_ref[pl.ds(d * tiles, tiles), j].reshape(part, tokens)
            out[j * part : (j + 1) * part] = nt(low, g).astype(bf16)
            rows = hid_ref[j, pl.ds(pl.multiple_of(d * deep, deep), deep)]
            base = 2 * part + j * deep
            out[base : base + deep] = nt(rows, grad_down).astype(bf16)
            low = mixed_ref[pl.ds(d * tiles, tiles), j].reshape(part, tokens)
            base = 2 * part + 2 * deep + j * hidden * part // width
            for q in range(hidden // width):
                grads = gp_ref[j, q * width : (q + 1) * width]
                out[base + q * part : base + (q + 1) * part] = nt(low, grads).astype(bf16)


def first_terms_kernel(dp_ref, xt_ref, gf_ref, *outs):
    shares = len(outs)
    width = xt_ref.shape[1]
    part = width // shares
    for i in range(2):
        grad_first = unpack(gf_ref, i)
        for k in range(shares):
            d = lax.rem(dp_ref[0] + k, shares)
            rows = xt_ref[i, pl.ds(pl.multiple_of(d * part, part), part)]
            outs[k][i * part : (i + 1) * part] = nt(rows, grad_first).astype(bf16)


def main_sum_kernel(*refs, factor):
    parts, (second_ref, down_ref, last_ref) = refs[:-3], refs[-3:]
    part, width = last_ref.shape[1:]
    deep = down_ref.shape[1]
    hidden = second_ref.shape[2]

    def total(base, count):
        value = parts[0][base : base + count].astype(f32)
        for ref in parts[1:]:
            value = value + ref[base : base + count].astype(f32)
        return value * factor

    for j in range(2):
        last_ref[j] = total(j * part, part)
        down_ref[j] = total(2 * part + j * deep, deep)
        base = 2 * part + 2 * deep + j * hidden * part // width
        for q in range(hidden // width):
            second_ref[j, :, q * width : (q + 1) * width] = total(base + q * part, part)


def first_sum_kernel(*refs, factor):
    parts, out_ref = refs[:-1], refs[-1]
    part = out_ref.shape[1]
    for i in range(2):
        value = parts[0][i * part : (i + 1) * part].astype(f32)
        for ref in parts[1:]:
            value = value + ref[i * part : (i + 1) * part].astype(f32)
        out_ref[i] = value * factor


def shuffle(value):
    return lax.all_to_all(value, "tensor", split_axis=0, concat_axis=0, tiled=True)


def spread(chunks):
    shares = len(chunks)
    moved = [chunks[0]]
    for k in range(1, shares):
        pairs = [(i, (i + k) % shares) for i in range(shares)]
        moved.append(lax.ppermute(chunks[k], "dp", pairs))
    return moved


def body(inputs, cotangent, up_first, up_second, down_first, down_second):
    x, u1, u2, d1, d2 = (inputs[0], up_first[0], up_second[0], down_first[0], down_second[0])
    tokens = x.shape[0]
    _, width, hidden = u2.shape
    peers = lax.axis_size("tensor")
    shares = lax.axis_size("dp")
    sections = lax.axis_size("pipe")
    section = lax.axis_index("pipe")
    dp_at = lax.axis_index("dp").astype(jnp.int32).reshape(1)
    is_last = (section == sections - 1).astype(jnp.int32).reshape(1)
    factor = 1.0 / math.sqrt(tokens * shares)
    part, deep = width // shares, hidden // shares
    packet = struct((peers, 2, 16, tokens))
    wide = struct((2, width, tokens))
    tall = struct((2, hidden, tokens))
    block = 2 * 2 * width * tokens * width
    big = 2 * 2 * width * tokens * hidden

    def head(gt):
        return call(head_kernel, [packet], (gt, d2), block)[0]

    def tail(r, gt):
        return call(tail_kernel, [wide], (r, gt, u1), block)[0]

    def main_terms(last, gt, gd, at, gp):
        rows = 2 * part + 2 * deep + 2 * hidden * part // width
        return call(
            functools.partial(main_terms_kernel, at=at),
            [struct((rows, width))] * shares,
            (dp_at, last, gt, hid, gd, r0, gp),
            block + 2 * big,
            1,
        )

    def first_terms(gf):
        return call(first_terms_kernel, [struct((2 * part, width))] * shares, (dp_at, xt, gf), block, 1)

    def main_sum(parts):
        return call(
            functools.partial(main_sum_kernel, factor=factor),
            [struct((2, part, hidden), f32), struct((2, deep, width), f32), struct((2, part, width), f32)],
            parts,
        )

    def first_sum(parts):
        return call(
            functools.partial(first_sum_kernel, factor=factor), [struct((2, part, width), f32)], parts
        )[0]

    def finish(last, gt, gd, at, gp, gf, out):
        second, down, low = main_sum(spread(main_terms(last, gt, gd, at, gp)))
        first = first_sum(spread(first_terms(gf)))
        rows = call(rows_kernel, [struct((tokens, 2 * width))], (out,))[0]
        return rows, first, second, down, low

    sent = call(
        entry_kernel, [struct((peers, 4, 16, tokens))], (x, cotangent, u1, d2), 2 * block
    )[0]
    r0 = shuffle(sent)
    xt, gt3 = call(turn_kernel, [wide, wide], (x, cotangent))
    u2t, d1t = call(
        flip_kernel, [struct((2, hidden, width)), struct((2, width, hidden))], (u2, d1)
    )
    sent, slope, hid, gp3 = call(
        forward_kernel,
        [packet, struct((2, hidden, tokens), f32), tall, tall],
        (is_last, r0, u2t, d1t, d1, u2),
        3 * big,
        1,
    )
    r1 = shuffle(sent)
    out3 = tail(r1, gt3)

    def no_done():
        return (
            jnp.zeros((tokens, 2 * width), bf16),
            jnp.zeros((2, part, width), f32),
            jnp.zeros((2, part, hidden), f32),
            jnp.zeros((2, deep, width), f32),
            jnp.zeros((2, part, width), f32),
        )

    def no_chain():
        return (
            jnp.zeros(wide.shape, bf16),
            jnp.zeros(packet.shape, bf16),
            jnp.zeros(tall.shape, bf16),
            jnp.zeros(packet.shape, bf16),
        )

    def chain(gt):
        gd = shuffle(head(gt))
        sent, gp = call(middle_kernel, [packet, tall], (gd, slope, d1, u2), 2 * big)
        gf = shuffle(sent)
        return tail(gf, gt), gd, gp, gf

    def hand(value, source):
        return lax.ppermute(value, "pipe", [(source, source - 1)])

    def choose(turn, idle, active, closing):
        at = jnp.where(
            section == sections - 1 - turn, 1, jnp.where(section == sections - turn, 2, 0)
        )
        return lax.switch(at, [idle, active, closing])

    g2 = hand(out3, 3)

    def closing3():
        sent = call(down_kernel, [packet], (hid, d1t), big)[0]
        return no_chain(), finish(shuffle(sent), gt3, r0, 2, gp3, r1, out3)

    chain2, done = choose(
        1,
        lambda: (no_chain(), no_done()),
        lambda: (chain(g2), no_done()),
        closing3,
    )
    g1 = hand(chain2[0], 2)
    done3 = done
    chain1, done = choose(
        2,
        lambda: (no_chain(), done3),
        lambda: (chain(g1), no_done()),
        lambda: (no_chain(), finish(r1, g2, chain2[1], 0, chain2[2], chain2[3], chain2[0])),
    )
    g0 = hand(chain1[0], 1)
    done2 = done

    def closing0():
        gd = shuffle(head(g0))
        sent, gp = call(middle_kernel, [packet, tall], (gd, slope, d1, u2), 2 * big)
        moved = spread(main_terms(r1, g0, gd, 0, gp))
        gf = shuffle(sent)
        first_moved = spread(first_terms(gf))
        rows = call(rows_kernel, [struct((tokens, 2 * width))], (tail(gf, g0),))[0]
        second, down, low = main_sum(moved)
        return rows, first_sum(first_moved), second, down, low

    done = choose(
        3,
        lambda: done2,
        closing0,
        lambda: finish(r1, g1, chain1[1], 0, chain1[2], chain1[3], chain1[0]),
    )
    rows, first, second, down, low = done
    return (rows[None], first[None], second[None], down[None], low[None])


def solution(mesh):
    return jax.shard_map(
        body,
        mesh=mesh,
        in_specs=(
            P("pipe", "dp", "tensor"),
            P("dp", "tensor"),
            P("pipe", "tensor", None, None),
            P("pipe", "tensor", None, None),
            P("pipe", "tensor", None, None),
            P("pipe", "tensor", None, None),
        ),
        out_specs=(
            P("pipe", "dp", "tensor"),
            P("pipe", "tensor", "dp", None),
            P("pipe", "tensor", "dp", None),
            P("pipe", "tensor", "dp", None),
            P("pipe", "tensor", "dp", None),
        ),
        check_vma=False,
    )
```

```python
import functools
import math

import jax
import jax.numpy as jnp
from jax import lax
from jax.experimental import pallas as pl
from jax.experimental.pallas import tpu as pltpu
from jax.sharding import PartitionSpec as P

root_half = 1.0 / math.sqrt(2.0)
norm_density = 1.0 / math.sqrt(2.0 * math.pi)
f32 = jnp.float32
bf16 = jnp.bfloat16


def dot(a, b, dims):
    return lax.dot_general(a, b, (dims, ((), ())), preferred_element_type=f32)


def nn(a, b):
    return dot(a, b, ((1,), (0,)))


def nt(a, b):
    return dot(a, b, ((1,), (1,)))


def tn(a, b):
    return dot(a, b, ((0,), (0,)))


def pack(out_ref, at, parts, tokens):
    lanes = parts[0].shape[1] // 2
    extra = tokens - lanes
    peers = out_ref.shape[0]
    groups = []
    shaped = [part.reshape(peers, 2, 8, 2 * lanes) for part in parts]
    for block in range(2):
        for local in range(2):
            groups.append(shaped[local][:, block])
    lane = lax.broadcasted_iota(jnp.int32, (peers * 8, lanes), 1)
    last = groups[3][..., lanes:].reshape(peers * 8, lanes)
    for n, group in enumerate(groups):
        out_ref[:, at + n] = group[..., :lanes].astype(bf16)
        if n < 3:
            rest = group[..., lanes:].reshape(peers * 8, lanes)
            moved = pltpu.roll(last, extra - n * (lanes - extra), 1)
            joined = jnp.where(lane < extra, rest, moved)
            out_ref[:, at + 4 + n] = joined.reshape(peers, 8, lanes).astype(bf16)


def unpack(ref, at, block, tokens):
    peers, _, _, lanes = ref.shape
    extra = tokens - lanes
    lane = lax.broadcasted_iota(jnp.int32, (peers * 8, lanes), 1)

    def group(n):
        return ref[:, at + n].astype(f32)

    parts = []
    for n in (2 * block, 2 * block + 1):
        if n < 3:
            rest = jnp.where(lane < extra, group(4 + n).reshape(peers * 8, lanes), 0.0)
        else:
            rest = jnp.zeros((peers * 8, lanes), f32)
            for m in range(3):
                low = m * (lanes - extra)
                piece = pltpu.roll(
                    group(4 + m).reshape(peers * 8, lanes), (low + lanes - extra) % lanes, 1
                )
                inside = (lane >= low) & (lane < low + lanes - extra)
                rest = jnp.where(inside, piece, rest)
        parts.append(jnp.concatenate([group(n), rest.reshape(peers, 8, lanes)], axis=2))
    joined = jnp.stack(parts, axis=1)
    return joined.reshape(peers * 16, 2 * lanes).astype(bf16)


def near(value):
    return pltpu.with_memory_space_constraint(value, pltpu.VMEM)


def held(value):
    return pltpu.VMEM(value.shape, value.dtype)


def call(body, outs, args, flops=0, scalars=0, scratch=(), room=12):
    moved = sum(a.size * a.dtype.itemsize for a in args) + sum(
        math.prod(o.shape) * o.dtype.itemsize for o in outs
    )
    specs = [pl.BlockSpec(memory_space=pltpu.SMEM)] * scalars
    specs += [pl.BlockSpec(memory_space=pltpu.VMEM)] * (len(args) - scalars)
    return pl.pallas_call(
        body,
        out_shape=outs,
        scratch_shapes=scratch,
        in_specs=specs,
        out_specs=[pl.BlockSpec(memory_space=pltpu.VMEM)] * len(outs),
        compiler_params=pltpu.CompilerParams(vmem_limit_bytes=room * 2**20),
        cost_estimate=pl.CostEstimate(flops=flops, bytes_accessed=moved, transcendentals=0),
    )(*args)


def struct(shape, dtype=bf16):
    return jax.ShapeDtypeStruct(shape, dtype)


def padded(value, rows):
    zeros = jnp.zeros((rows - value.shape[0], value.shape[1]), value.dtype)
    return jnp.concatenate([value, zeros], axis=0)


def stage_kernel(*refs):
    half = len(refs) // 2
    for source, target in zip(refs[:half], refs[half:]):
        target[...] = source[...]


def entry_kernel(x_ref, g_ref, u1_ref, d2_ref, out_ref, u1_near, d2_near):
    u1_near[...] = u1_ref[...]
    d2_near[...] = d2_ref[...]
    tokens, lanes = x_ref.shape[0], 2 * out_ref.shape[3]
    width = u1_ref.shape[1]
    firsts, lasts = [], []
    for i in range(2):
        cols = slice(i * width, (i + 1) * width)
        firsts.append(nn(padded(x_ref[:, cols], lanes), u1_ref[i]).T)
        lasts.append(nt(d2_ref[i], padded(g_ref[:, cols], lanes)))
    pack(out_ref, 0, firsts, tokens)
    pack(out_ref, 7, lasts, tokens)


def forward_kernel(
    last_ref, r_ref, d1_ref, u2_ref, out_ref, slope_ref, hid_ref, gd_ref, *, tokens
):
    hidden = d1_ref.shape[1]
    step = 256
    for j in range(2):
        mixed = unpack(r_ref, 0, j, tokens)
        for h in range(0, hidden, step):
            pre = tn(u2_ref[j, :, h : h + step], mixed)
            cumulative = 0.5 * (1.0 + lax.erf(pre * root_half))
            hid_ref[j, h : h + step] = (pre * cumulative).astype(bf16)
            density = jnp.exp(-0.5 * pre * pre) * norm_density
            slope_ref[j, h : h + step] = (cumulative + pre * density).astype(bf16)
    gd_ref[...] = r_ref[:, 7:14]

    @pl.when(last_ref[0] == 1)
    def _():
        backward(gd_ref, slope_ref, d1_ref, u2_ref, out_ref, tokens)

    @pl.when(last_ref[0] == 0)
    def _():
        pack(out_ref, 0, [tn(d1_ref[j], hid_ref[j]) for j in range(2)], tokens)


def backward(r_ref, slope_ref, d1_ref, u2_ref, out_ref, tokens):
    step = 256
    mixes = []
    for j in range(2):
        grad_down = unpack(r_ref, 0, j, tokens)
        grads = []
        for h in range(0, d1_ref.shape[1], step):
            grad_hidden = nn(d1_ref[j, h : h + step], grad_down)
            grads.append((grad_hidden * slope_ref[j, h : h + step]).astype(bf16))
        mixes.append(nn(u2_ref[j], jnp.concatenate(grads, axis=0)))
    pack(out_ref, 0, mixes, tokens)


def middle_kernel(r_ref, slope_ref, d1_ref, u2_ref, out_ref, *, tokens):
    backward(r_ref, slope_ref, d1_ref, u2_ref, out_ref, tokens)


def down_kernel(hid_ref, d1_ref, out_ref, *, tokens):
    pack(out_ref, 0, [tn(d1_ref[j], hid_ref[j]) for j in range(2)], tokens)


def head_kernel(g_ref, d2_ref, out_ref):
    tokens, lanes = g_ref.shape[0], 2 * out_ref.shape[3]
    width = d2_ref.shape[1]
    parts = []
    for i in range(2):
        rows = padded(g_ref[:, i * width : (i + 1) * width], lanes)
        parts.append(nt(d2_ref[i], rows))
    pack(out_ref, 0, parts, tokens)


def tail_kernel(r_ref, g_ref, u1_ref, out_ref):
    tokens = g_ref.shape[0]
    width = u1_ref.shape[1]
    for i in range(2):
        cols = slice(i * width, (i + 1) * width)
        acts = nn(u1_ref[i], unpack(r_ref, 0, i, tokens)).T[:tokens]
        out_ref[:, cols] = (g_ref[:, cols].astype(f32) + acts).astype(bf16)


def main_terms_kernel(
    dp_ref, last_ref, g_ref, hid_ref, gd_ref, mixed_ref, slope_ref, d1_ref, *rest
):
    outs, low_ref = rest[:-1], rest[-1]
    tokens = g_ref.shape[0]
    shares = len(outs)
    hidden, lanes = hid_ref.shape[1:]
    width = g_ref.shape[1] // 2
    part, deep = width // shares, hidden // shares
    for j in range(2):
        g = padded(g_ref[:, j * width : (j + 1) * width], lanes)
        grad_down = unpack(gd_ref, 0, j, tokens)
        low_ref[0] = unpack(last_ref, 0, j, tokens)
        low_ref[1] = unpack(mixed_ref, 0, j, tokens)
        grads = []
        for q in range(hidden // width):
            span = slice(q * width, (q + 1) * width)
            grad_hidden = nn(d1_ref[j, span], grad_down)
            grads.append((grad_hidden * slope_ref[j, span]).astype(bf16))
        for k in range(shares):
            d = lax.rem(dp_ref[0] + k, shares)
            out = outs[k]
            span = pl.ds(pl.multiple_of(d * part, part), part)
            low = low_ref[0, span]
            out[j * part : (j + 1) * part] = nn(low, g).astype(bf16)
            rows = hid_ref[j, pl.ds(pl.multiple_of(d * deep, deep), deep)]
            base = 2 * part + j * deep
            out[base : base + deep] = nt(rows, grad_down).astype(bf16)
            low = low_ref[1, span]
            base = 2 * part + 2 * deep + j * hidden * part // width
            for q in range(hidden // width):
                out[base + q * part : base + (q + 1) * part] = nt(low, grads[q]).astype(bf16)


def first_terms_kernel(dp_ref, x_ref, gf_ref, *rest):
    outs, xt_ref = rest[:-1], rest[-1]
    shares = len(outs)
    width, lanes = xt_ref.shape[1:]
    part = width // shares
    for i in range(2):
        grad_first = unpack(gf_ref, 0, i, x_ref.shape[0])
        rows = padded(x_ref[:, i * width : (i + 1) * width], lanes)
        xt_ref[i] = rows.astype(f32).T.astype(bf16)
        for k in range(shares):
            d = lax.rem(dp_ref[0] + k, shares)
            rows = xt_ref[i, pl.ds(pl.multiple_of(d * part, part), part)]
            outs[k][i * part : (i + 1) * part] = nt(rows, grad_first).astype(bf16)


def main_sum_kernel(*refs, factor):
    parts, (second_ref, down_ref, last_ref) = refs[:-3], refs[-3:]
    part, width = last_ref.shape[1:]
    deep = down_ref.shape[1]
    hidden = second_ref.shape[2]

    def total(base, count):
        value = parts[0][base : base + count].astype(f32)
        for ref in parts[1:]:
            value = value + ref[base : base + count].astype(f32)
        return value * factor

    for j in range(2):
        last_ref[j] = total(j * part, part)
        down_ref[j] = total(2 * part + j * deep, deep)
        base = 2 * part + 2 * deep + j * hidden * part // width
        for q in range(hidden // width):
            second_ref[j, :, q * width : (q + 1) * width] = total(base + q * part, part)


def first_sum_kernel(*refs, factor):
    parts, out_ref = refs[:-1], refs[-1]
    part = out_ref.shape[1]
    for i in range(2):
        value = parts[0][i * part : (i + 1) * part].astype(f32)
        for ref in parts[1:]:
            value = value + ref[i * part : (i + 1) * part].astype(f32)
        out_ref[i] = value * factor


def shuffle(value):
    return lax.all_to_all(value, "tensor", split_axis=0, concat_axis=0, tiled=True)


def spread(chunks):
    shares = len(chunks)
    moved = [chunks[0]]
    for k in range(1, shares):
        pairs = [(i, (i + k) % shares) for i in range(shares)]
        moved.append(lax.ppermute(chunks[k], "dp", pairs))
    return moved


def body(inputs, cotangent, up_first, up_second, down_first, down_second):
    x, u1, u2, d1, d2 = (inputs[0], up_first[0], up_second[0], down_first[0], down_second[0])
    tokens = x.shape[0]
    _, width, hidden = u2.shape
    peers = lax.axis_size("tensor")
    shares = lax.axis_size("dp")
    sections = lax.axis_size("pipe")
    section = lax.axis_index("pipe")
    dp_at = lax.axis_index("dp").astype(jnp.int32).reshape(1)
    is_last = (section == sections - 1).astype(jnp.int32).reshape(1)
    factor = 1.0 / math.sqrt(tokens * shares)
    part, deep = width // shares, hidden // shares
    lanes = -(-tokens // 128) * 128
    packet = struct((peers, 7, 8, 128))
    rows = struct((tokens, 2 * width))
    tall = struct((2, hidden, lanes))
    block = 2 * 2 * width * lanes * width
    big = 2 * 2 * width * lanes * hidden

    def head(g):
        return call(head_kernel, [held(packet)], (g, d2), block)[0]

    def tail(r, g):
        return call(tail_kernel, [held(rows)], (r, g, u1), block)[0]

    def middle(gd):
        return call(
            functools.partial(middle_kernel, tokens=tokens), [held(packet)], (gd, slope, d1, u2), 2 * big
        )[0]

    def main_terms(last, g, gd):
        count = 2 * part + 2 * deep + 2 * hidden * part // width
        return call(
            main_terms_kernel,
            [struct((count, width))] * shares,
            (dp_at, last, g, hid, gd, r0, slope, d1),
            block + 3 * big,
            1,
            scratch=[pltpu.VMEM((2, width, lanes), bf16)],
        )

    def first_terms(gf):
        return call(
            first_terms_kernel,
            [struct((2 * part, width))] * shares,
            (dp_at, x, gf),
            block,
            1,
            scratch=[pltpu.VMEM((2, width, lanes), bf16)],
        )

    def main_sum(parts):
        return call(
            functools.partial(main_sum_kernel, factor=factor),
            [struct((2, part, hidden), f32), struct((2, deep, width), f32), struct((2, part, width), f32)],
            parts,
        )

    def first_sum(parts):
        return call(
            functools.partial(first_sum_kernel, factor=factor), [struct((2, part, width), f32)], parts
        )[0]

    def finish(last, g, gd, gf, out):
        moved = spread(main_terms(last, g, gd))
        first_moved = spread(first_terms(gf))
        second, down, low = main_sum(moved)
        return out, first_sum(first_moved), second, down, low

    sent, u1, d2 = call(
        entry_kernel,
        [struct((peers, 14, 8, 128)), held(u1), held(d2)],
        (x, cotangent, u1, d2),
        2 * block,
        room=56,
    )
    d1, u2 = call(stage_kernel, [held(d1), held(u2)], (d1, u2))
    u1, d2, d1, u2 = near(u1), near(d2), near(d1), near(u2)
    r0 = shuffle(sent)
    sent, slope, hid, gd3 = call(
        functools.partial(forward_kernel, tokens=tokens),
        [held(packet), tall, tall, packet],
        (is_last, r0, d1, u2),
        3 * big,
        1,
    )

    r1 = shuffle(sent)
    out3 = tail(r1, cotangent)

    def chain(g):
        gd = shuffle(head(g))
        gf = shuffle(middle(gd))
        return tail(gf, g), gd, gf

    def nothing():
        shapes = (rows, packet, packet)
        return tuple(jnp.zeros(s.shape, s.dtype) for s in shapes)

    def hand(value, source):
        return lax.ppermute(value, "pipe", [(source, source - 1)])

    g2 = hand(out3, 3)
    g2_near = near(g2)
    saved2 = lax.cond(section == 2, lambda: chain(g2_near), nothing)
    g1 = hand(saved2[0], 2)
    g1_near = near(g1)
    saved = lax.cond(section == 1, lambda: chain(g1_near), lambda: saved2)
    g0 = near(hand(saved[0], 1))

    def last_turn():
        gd = shuffle(head(g0))
        sent = middle(gd)
        moved = spread(main_terms(r1, g0, gd))
        gf = shuffle(sent)
        first_moved = spread(first_terms(gf))
        out = tail(gf, g0)
        second, down, low = main_sum(moved)
        return out, first_sum(first_moved), second, down, low

    def close_middle():
        out, gd, gf = saved
        return finish(r1, jnp.where(section == 1, g1, g2), gd, gf, out)

    def close_top():
        sent = call(functools.partial(down_kernel, tokens=tokens), [packet], (hid, d1), big)[0]
        return finish(shuffle(sent), cotangent, gd3, r1, out3)

    branch = jnp.where(section == 0, 0, jnp.where(section == sections - 1, 2, 1))
    done = lax.switch(branch, [last_turn, close_middle, close_top])
    out, first, second, down, low = done
    return (out[None], first[None], second[None], down[None], low[None])


def solution(mesh):
    return jax.shard_map(
        body,
        mesh=mesh,
        in_specs=(
            P("pipe", "dp", "tensor"),
            P("dp", "tensor"),
            P("pipe", "tensor", None, None),
            P("pipe", "tensor", None, None),
            P("pipe", "tensor", None, None),
            P("pipe", "tensor", None, None),
        ),
        out_specs=(
            P("pipe", "dp", "tensor"),
            P("pipe", "tensor", "dp", None),
            P("pipe", "tensor", "dp", None),
            P("pipe", "tensor", "dp", None),
            P("pipe", "tensor", "dp", None),
        ),
        check_vma=False,
    )
```

```python
import functools
import math

import jax
import jax.numpy as jnp
from jax import lax
from jax.experimental import pallas as pl
from jax.experimental.pallas import tpu as pltpu
from jax.sharding import PartitionSpec as P


root_half = 1.0 / math.sqrt(2.0)
norm_density = 1.0 / math.sqrt(2.0 * math.pi)
f32 = jnp.float32
bf16 = jnp.bfloat16


def dot(a, b, dims):
    return lax.dot_general(a, b, (dims, ((), ())), preferred_element_type=f32)


def nn(a, b):
    return dot(a, b, ((1,), (0,)))


def nt(a, b):
    return dot(a, b, ((1,), (1,)))


def tn(a, b):
    return dot(a, b, ((0,), (0,)))


def pack(out_ref, at, parts, tokens):
    lanes = parts[0].shape[1] // 2
    extra = tokens - lanes
    peers = out_ref.shape[0]
    groups = []
    shaped = [part.reshape(peers, 2, 8, 2 * lanes) for part in parts]
    for block in range(2):
        for local in range(2):
            groups.append(shaped[local][:, block])
    lane = lax.broadcasted_iota(jnp.int32, (peers * 8, lanes), 1)
    last = groups[3][..., lanes:].reshape(peers * 8, lanes)
    for n, group in enumerate(groups):
        out_ref[:, at + n] = group[..., :lanes].astype(bf16)
        if n < 3:
            rest = group[..., lanes:].reshape(peers * 8, lanes)
            moved = pltpu.roll(last, extra - n * (lanes - extra), 1)
            joined = jnp.where(lane < extra, rest, moved)
            out_ref[:, at + 4 + n] = joined.reshape(peers, 8, lanes).astype(bf16)


def unpack(ref, at, block, tokens):
    peers, _, _, lanes = ref.shape
    extra = tokens - lanes
    lane = lax.broadcasted_iota(jnp.int32, (peers * 8, lanes), 1)

    def group(n):
        return ref[:, at + n].astype(f32)

    parts = []
    for n in (2 * block, 2 * block + 1):
        if n < 3:
            rest = jnp.where(lane < extra, group(4 + n).reshape(peers * 8, lanes), 0.0)
        else:
            rest = jnp.zeros((peers * 8, lanes), f32)
            for m in range(3):
                low = m * (lanes - extra)
                piece = pltpu.roll(
                    group(4 + m).reshape(peers * 8, lanes), (low + lanes - extra) % lanes, 1
                )
                inside = (lane >= low) & (lane < low + lanes - extra)
                rest = jnp.where(inside, piece, rest)
        parts.append(jnp.concatenate([group(n), rest.reshape(peers, 8, lanes)], axis=2))
    joined = jnp.stack(parts, axis=1)
    return joined.reshape(peers * 16, 2 * lanes).astype(bf16)


def near(value):
    return pltpu.with_memory_space_constraint(value, pltpu.VMEM)


def held(value):
    return pltpu.VMEM(value.shape, value.dtype)


def call(body, outs, args, flops=0, scalars=0, scratch=(), room=12):
    moved = sum(a.size * a.dtype.itemsize for a in args) + sum(
        math.prod(o.shape) * o.dtype.itemsize for o in outs
    )
    specs = [pl.BlockSpec(memory_space=pltpu.SMEM)] * scalars
    specs += [pl.BlockSpec(memory_space=pltpu.VMEM)] * (len(args) - scalars)
    return pl.pallas_call(
        body,
        out_shape=outs,
        scratch_shapes=scratch,
        in_specs=specs,
        out_specs=[pl.BlockSpec(memory_space=pltpu.VMEM)] * len(outs),
        compiler_params=pltpu.CompilerParams(vmem_limit_bytes=room * 2**20),
        cost_estimate=pl.CostEstimate(flops=flops, bytes_accessed=moved, transcendentals=0),
    )(*args)


def struct(shape, dtype=bf16):
    return jax.ShapeDtypeStruct(shape, dtype)


def padded(value, rows):
    zeros = jnp.zeros((rows - value.shape[0], value.shape[1]), value.dtype)
    return jnp.concatenate([value, zeros], axis=0)


def stage_kernel(*refs):
    half = len(refs) // 2
    for source, target in zip(refs[:half], refs[half:]):
        target[...] = source[...]


def first_parts(x_ref, u1_ref, lanes):
    width = u1_ref.shape[1]
    parts = []
    for i in range(2):
        cols = slice(i * width, (i + 1) * width)
        parts.append(nn(padded(x_ref[:, cols], lanes), u1_ref[i]).T)
    return parts


def last_parts(g_ref, d2_ref, lanes):
    width = d2_ref.shape[1]
    parts = []
    for i in range(2):
        cols = slice(i * width, (i + 1) * width)
        parts.append(nt(d2_ref[i], padded(g_ref[:, cols], lanes)))
    return parts


def entry_kernel(x_ref, u1_ref, out_ref):
    pack(out_ref, 0, first_parts(x_ref, u1_ref, 2 * out_ref.shape[3]), x_ref.shape[0])


def top_entry_kernel(x_ref, g_ref, u1_ref, d2_ref, out_ref):
    lanes = 2 * out_ref.shape[3]
    pack(out_ref, 0, first_parts(x_ref, u1_ref, lanes), x_ref.shape[0])
    pack(out_ref, 7, last_parts(g_ref, d2_ref, lanes), x_ref.shape[0])


def activate(r_ref, u2_ref, slope_ref, hid_ref, tokens):
    hidden = u2_ref.shape[2]
    step = 256
    for j in range(2):
        mixed = unpack(r_ref, 0, j, tokens)
        for h in range(0, hidden, step):
            pre = tn(u2_ref[j, :, h : h + step], mixed)
            cumulative = 0.5 * (1.0 + lax.erf(pre * root_half))
            hid_ref[j, h : h + step] = (pre * cumulative).astype(bf16)
            density = jnp.exp(-0.5 * pre * pre) * norm_density
            slope_ref[j, h : h + step] = (cumulative + pre * density).astype(bf16)


def forward_kernel(r_ref, d1_ref, u2_ref, out_ref, slope_ref, hid_ref, *, tokens):
    activate(r_ref, u2_ref, slope_ref, hid_ref, tokens)
    pack(out_ref, 0, [tn(d1_ref[j], hid_ref[j]) for j in range(2)], tokens)


def top_kernel(
    r_ref, d1_ref, u2_ref, out_ref, slope_ref, hid_ref, mixed_ref, gd_ref, *, tokens
):
    activate(r_ref, u2_ref, slope_ref, hid_ref, tokens)
    mixed_ref[...] = r_ref[:, :7]
    gd_ref[...] = r_ref[:, 7:]
    backward(gd_ref, slope_ref, d1_ref, u2_ref, out_ref, tokens)


def backward(r_ref, slope_ref, d1_ref, u2_ref, out_ref, tokens):
    step = 256
    mixes = []
    for j in range(2):
        grad_down = unpack(r_ref, 0, j, tokens)
        grads = []
        for h in range(0, d1_ref.shape[1], step):
            grad_hidden = nn(d1_ref[j, h : h + step], grad_down)
            grads.append((grad_hidden * slope_ref[j, h : h + step]).astype(bf16))
        mixes.append(nn(u2_ref[j], jnp.concatenate(grads, axis=0)))
    pack(out_ref, 0, mixes, tokens)


def middle_kernel(r_ref, slope_ref, d1_ref, u2_ref, out_ref, *, tokens):
    backward(r_ref, slope_ref, d1_ref, u2_ref, out_ref, tokens)


def down_kernel(hid_ref, d1_ref, out_ref, *, tokens):
    pack(out_ref, 0, [tn(d1_ref[j], hid_ref[j]) for j in range(2)], tokens)


def head_kernel(g_ref, d2_ref, out_ref):
    pack(out_ref, 0, last_parts(g_ref, d2_ref, 2 * out_ref.shape[3]), g_ref.shape[0])


def tail_kernel(r_ref, g_ref, u1_ref, out_ref):
    tokens = g_ref.shape[0]
    width = u1_ref.shape[1]
    for i in range(2):
        cols = slice(i * width, (i + 1) * width)
        acts = nn(u1_ref[i], unpack(r_ref, 0, i, tokens)).T[:tokens]
        out_ref[:, cols] = (g_ref[:, cols].astype(f32) + acts).astype(bf16)


def main_terms_kernel(
    dp_ref, last_ref, g_ref, hid_ref, gd_ref, mixed_ref, slope_ref, d1_ref, *rest
):
    outs, low_ref = rest[:-1], rest[-1]
    tokens = g_ref.shape[0]
    hidden, lanes = hid_ref.shape[1:]
    width = g_ref.shape[1] // 2
    shares = len(outs)
    part, deep = width // shares, hidden // shares
    half = outs[0].shape[0] // 2

    def put(k, base, value):
        outs[k][base : base + value.shape[0]] = value.astype(bf16)

    def turned(n):
        spans = []
        for k in range(shares):
            d = lax.rem(dp_ref[0] + k, shares)
            spans.append(low_ref[n, pl.ds(pl.multiple_of(d * part, part), part)])
        return jnp.concatenate(spans, axis=0)

    for j in range(2):
        g = padded(g_ref[:, j * width : (j + 1) * width], lanes)
        grad_down = unpack(gd_ref, 0, j, tokens)
        low_ref[0] = unpack(last_ref, 0, j, tokens)
        low_ref[1] = unpack(mixed_ref, 0, j, tokens)
        start = j * half
        lows = nn(turned(0), g)
        for k in range(shares):
            put(k, start, lows[k * part : (k + 1) * part])
        for k in range(shares):
            d = lax.rem(dp_ref[0] + k, shares)
            rows = hid_ref[j, pl.ds(pl.multiple_of(d * deep, deep), deep)]
            put(k, start + part, nt(rows, grad_down))
        mixed = turned(1)
        for q in range(hidden // width):
            span = slice(q * width, (q + 1) * width)
            grad_hidden = nn(d1_ref[j, span], grad_down)
            grads = (grad_hidden * slope_ref[j, span]).astype(bf16)
            terms = nt(mixed, grads)
            for k in range(shares):
                put(k, start + part + deep + q * part, terms[k * part : (k + 1) * part])


def first_terms_kernel(dp_ref, x_ref, gf_ref, *rest):
    outs, xt_ref = rest[:-1], rest[-1]
    shares = len(outs)
    width, lanes = xt_ref.shape[1:]
    part = width // shares
    for i in range(2):
        grad_first = unpack(gf_ref, 0, i, x_ref.shape[0])
        rows = padded(x_ref[:, i * width : (i + 1) * width], lanes)
        xt_ref[i] = rows.astype(f32).T.astype(bf16)
        for k in range(shares):
            d = lax.rem(dp_ref[0] + k, shares)
            rows = xt_ref[i, pl.ds(pl.multiple_of(d * part, part), part)]
            outs[k][i * part : (i + 1) * part] = nt(rows, grad_first).astype(bf16)


def main_sum_kernel(*refs, factor):
    parts, (second_ref, down_ref, last_ref) = refs[:-3], refs[-3:]
    part, width = last_ref.shape[1:]
    deep = down_ref.shape[1]
    hidden = second_ref.shape[2]
    half = parts[0].shape[0] // 2

    def total(base, count):
        value = parts[0][base : base + count].astype(f32)
        for ref in parts[1:]:
            value = value + ref[base : base + count].astype(f32)
        return value * factor

    for j in range(2):
        start = j * half
        last_ref[j] = total(start, part)
        down_ref[j] = total(start + part, deep)
        for q in range(hidden // width):
            at = start + part + deep + q * part
            second_ref[j, :, q * width : (q + 1) * width] = total(at, part)


def first_sum_kernel(*refs, factor):
    parts, out_ref = refs[:-1], refs[-1]
    part = out_ref.shape[1]
    for i in range(2):
        value = parts[0][i * part : (i + 1) * part].astype(f32)
        for ref in parts[1:]:
            value = value + ref[i * part : (i + 1) * part].astype(f32)
        out_ref[i] = value * factor


def shuffle(value):
    return lax.all_to_all(value, "tensor", split_axis=0, concat_axis=0, tiled=True)


def spread(chunks):
    shares = len(chunks)
    moved = [chunks[0]]
    for k in range(1, shares):
        pairs = [(i, (i + k) % shares) for i in range(shares)]
        moved.append(lax.ppermute(chunks[k], "dp", pairs))
    return moved


def body(inputs, cotangent, up_first, up_second, down_first, down_second):
    x, u1, u2, d1, d2 = (inputs[0], up_first[0], up_second[0], down_first[0], down_second[0])
    tokens = x.shape[0]
    _, width, hidden = u2.shape
    peers = lax.axis_size("tensor")
    shares = lax.axis_size("dp")
    sections = lax.axis_size("pipe")
    section = lax.axis_index("pipe")
    dp_at = lax.axis_index("dp").astype(jnp.int32).reshape(1)
    factor = 1.0 / math.sqrt(tokens * shares)
    part, deep = width // shares, hidden // shares
    lanes = -(-tokens // 128) * 128
    packet = struct((peers, 7, 8, 128))
    rows = struct((tokens, 2 * width))
    tall = struct((2, hidden, lanes))
    block = 2 * 2 * width * lanes * width
    big = 2 * 2 * width * lanes * hidden

    def head(g):
        return call(head_kernel, [held(packet)], (g, d2), block)[0]

    def tail(r, g):
        return call(tail_kernel, [held(rows)], (r, g, u1), block)[0]

    def middle(gd):
        return call(
            functools.partial(middle_kernel, tokens=tokens), [held(packet)], (gd, slope, d1, u2), 2 * big
        )[0]

    def main_moved(last, g, gd):
        count = 2 * (part + deep + hidden * part // width)
        chunks = call(
            main_terms_kernel,
            [struct((count, width))] * shares,
            (dp_at, last, g, hid, gd, mixed, slope, d1),
            block + 3 * big,
            1,
            scratch=[pltpu.VMEM((2, width, lanes), bf16)],
        )
        return spread(chunks)

    def first_terms(gf):
        return call(
            first_terms_kernel,
            [struct((2 * part, width))] * shares,
            (dp_at, x, gf),
            block,
            1,
            scratch=[pltpu.VMEM((2, width, lanes), bf16)],
        )

    def main_sum(parts):
        return call(
            functools.partial(main_sum_kernel, factor=factor),
            [struct((2, part, hidden), f32), struct((2, deep, width), f32), struct((2, part, width), f32)],
            parts,
        )

    def first_sum(parts):
        return call(
            functools.partial(first_sum_kernel, factor=factor), [struct((2, part, width), f32)], parts
        )[0]

    def finish(last, g, gd, gf, out):
        moved = main_moved(last, g, gd)
        first_moved = spread(first_terms(gf))
        second, down, low = main_sum(moved)
        return out, first_sum(first_moved), second, down, low

    def top():
        sent = call(
            top_entry_kernel,
            [struct((peers, 14, 8, 128))],
            (x, cotangent, up_first[0], down_second[0]),
            2 * block,
            room=56,
        )[0]
        sent, slope, hid, mixed, gd = call(
            functools.partial(top_kernel, tokens=tokens),
            [held(packet), tall, tall, packet, packet],
            (shuffle(sent), down_first[0], up_second[0]),
            3 * big,
        )
        gf = shuffle(sent)
        out = call(tail_kernel, [held(rows)], (gf, cotangent, up_first[0]), block)[0]
        return out, slope, hid, mixed, gf, gd

    def rest():
        sent = call(entry_kernel, [packet], (x, up_first[0]), block, room=56)[0]
        mixed = shuffle(sent)
        sent, slope, hid = call(
            functools.partial(forward_kernel, tokens=tokens),
            [held(packet), tall, tall],
            (mixed, down_first[0], up_second[0]),
            2 * big,
        )
        last = lax.cond(section == 2, lambda: sent, lambda: shuffle(sent))
        return jnp.zeros(rows.shape, bf16), slope, hid, mixed, last, jnp.zeros(packet.shape, bf16)

    out3, slope, hid, mixed, r1, gd3 = lax.cond(section == sections - 1, top, rest)
    u1, d2, d1, u2 = call(stage_kernel, [held(u1), held(d2), held(d1), held(u2)], (u1, d2, d1, u2))
    u1, d2, d1, u2 = near(u1), near(d2), near(d1), near(u2)

    def chain(g):
        gd = shuffle(head(g))
        gf = shuffle(middle(gd))
        return tail(gf, g), gd, gf

    def hand(value, source):
        return lax.ppermute(value, "pipe", [(source, source - 1)])

    g2 = hand(out3, 3)
    g2_near = near(g2)
    saved2 = lax.cond(section == 2, lambda: chain(g2_near), lambda: (out3, gd3, r1))
    g1 = hand(saved2[0], 2)
    g1_near = near(g1)
    saved = lax.cond(section == 1, lambda: chain(g1_near), lambda: saved2)
    g0 = near(hand(saved[0], 1))

    def last_turn():
        gd = shuffle(head(g0))
        sent = middle(gd)
        moved = main_moved(r1, g0, gd)
        gf = shuffle(sent)
        first_moved = spread(first_terms(gf))
        out = tail(gf, g0)
        second, down, low = main_sum(moved)
        return out, first_sum(first_moved), second, down, low

    def close(last):
        out, gd, gf = saved
        g = jnp.where(section == 3, cotangent, jnp.where(section == 2, g2, g1))
        return finish(last, g, gd, gf, out)

    def close_late():
        sent = call(functools.partial(down_kernel, tokens=tokens), [packet], (hid, d1), big)[0]
        return close(shuffle(sent))

    branch = jnp.where(section == 0, 0, jnp.where(section == 1, 1, 2))
    done = lax.switch(branch, [last_turn, lambda: close(r1), close_late])
    out, first, second, down, low = done
    return (out[None], first[None], second[None], down[None], low[None])


def solution(mesh):
    return jax.shard_map(
        body,
        mesh=mesh,
        in_specs=(
            P("pipe", "dp", "tensor"),
            P("dp", "tensor"),
            P("pipe", "tensor", None, None),
            P("pipe", "tensor", None, None),
            P("pipe", "tensor", None, None),
            P("pipe", "tensor", None, None),
        ),
        out_specs=(
            P("pipe", "dp", "tensor"),
            P("pipe", "tensor", "dp", None),
            P("pipe", "tensor", "dp", None),
            P("pipe", "tensor", "dp", None),
            P("pipe", "tensor", "dp", None),
        ),
        check_vma=False,
    )
```

```python
import functools
import math

import jax
import jax.numpy as jnp
from jax import lax
from jax.experimental import pallas as pl
from jax.experimental.pallas import tpu as pltpu
from jax.sharding import PartitionSpec as P


root_half = 1.0 / math.sqrt(2.0)
norm_density = 1.0 / math.sqrt(2.0 * math.pi)
f32 = jnp.float32
bf16 = jnp.bfloat16


def dot(a, b, dims):
    return lax.dot_general(a, b, (dims, ((), ())), preferred_element_type=f32)


def nn(a, b):
    return dot(a, b, ((1,), (0,)))


def nt(a, b):
    return dot(a, b, ((1,), (1,)))


def tn(a, b):
    return dot(a, b, ((0,), (0,)))


def pack(out_ref, at, parts, tokens):
    lanes = parts[0].shape[1] // 2
    extra = tokens - lanes
    peers = out_ref.shape[0]
    groups = []
    shaped = [part.reshape(peers, 2, 8, 2 * lanes) for part in parts]
    for block in range(2):
        for local in range(2):
            groups.append(shaped[local][:, block])
    lane = lax.broadcasted_iota(jnp.int32, (peers * 8, lanes), 1)
    last = groups[3][..., lanes:].reshape(peers * 8, lanes)
    for n, group in enumerate(groups):
        out_ref[:, at + n] = group[..., :lanes].astype(bf16)
        if n < 3:
            rest = group[..., lanes:].reshape(peers * 8, lanes)
            moved = pltpu.roll(last, extra - n * (lanes - extra), 1)
            joined = jnp.where(lane < extra, rest, moved)
            out_ref[:, at + 4 + n] = joined.reshape(peers, 8, lanes).astype(bf16)


def unpack(ref, at, block, tokens):
    peers, _, _, lanes = ref.shape
    extra = tokens - lanes
    lane = lax.broadcasted_iota(jnp.int32, (peers * 8, lanes), 1)

    def group(n):
        return ref[:, at + n].astype(f32)

    parts = []
    for n in (2 * block, 2 * block + 1):
        if n < 3:
            rest = jnp.where(lane < extra, group(4 + n).reshape(peers * 8, lanes), 0.0)
        else:
            rest = jnp.zeros((peers * 8, lanes), f32)
            for m in range(3):
                low = m * (lanes - extra)
                piece = pltpu.roll(
                    group(4 + m).reshape(peers * 8, lanes), (low + lanes - extra) % lanes, 1
                )
                inside = (lane >= low) & (lane < low + lanes - extra)
                rest = jnp.where(inside, piece, rest)
        parts.append(jnp.concatenate([group(n), rest.reshape(peers, 8, lanes)], axis=2))
    joined = jnp.stack(parts, axis=1)
    return joined.reshape(peers * 16, 2 * lanes).astype(bf16)


def near(value):
    return pltpu.with_memory_space_constraint(value, pltpu.VMEM)


def far(value):
    return pltpu.with_memory_space_constraint(value, pltpu.HBM)


def held(value):
    return pltpu.VMEM(value.shape, value.dtype)


def away(value):
    return pltpu.HBM(value.shape, value.dtype)


def call(body, outs, args, flops=0, scalars=0, scratch=(), room=8):
    moved = sum(a.size * a.dtype.itemsize for a in args) + sum(
        math.prod(o.shape) * o.dtype.itemsize for o in outs
    )
    specs = [pl.BlockSpec(memory_space=pltpu.SMEM)] * scalars
    specs += [pl.BlockSpec(memory_space=pltpu.VMEM)] * (len(args) - scalars)
    return pl.pallas_call(
        body,
        out_shape=outs,
        scratch_shapes=scratch,
        in_specs=specs,
        out_specs=[pl.BlockSpec(memory_space=pltpu.VMEM)] * len(outs),
        compiler_params=pltpu.CompilerParams(vmem_limit_bytes=room * 2**20),
        cost_estimate=pl.CostEstimate(flops=flops, bytes_accessed=moved, transcendentals=0),
    )(*args)


def struct(shape, dtype=bf16):
    return jax.ShapeDtypeStruct(shape, dtype)


def padded(value, rows):
    zeros = jnp.zeros((rows - value.shape[0], value.shape[1]), value.dtype)
    return jnp.concatenate([value, zeros], axis=0)


def stage_kernel(*refs):
    half = len(refs) // 2
    for source, target in zip(refs[:half], refs[half:]):
        target[...] = source[...]


def first_parts(x_ref, u1_ref, lanes):
    width = u1_ref.shape[1]
    parts = []
    for i in range(2):
        cols = slice(i * width, (i + 1) * width)
        parts.append(nn(padded(x_ref[:, cols], lanes), u1_ref[i]).T)
    return parts


def last_parts(g_ref, d2_ref, lanes):
    width = d2_ref.shape[1]
    parts = []
    for i in range(2):
        cols = slice(i * width, (i + 1) * width)
        parts.append(nt(d2_ref[i], padded(g_ref[:, cols], lanes)))
    return parts


def entry_kernel(x_ref, u1_ref, out_ref):
    pack(out_ref, 0, first_parts(x_ref, u1_ref, 2 * out_ref.shape[3]), x_ref.shape[0])


def top_entry_kernel(x_ref, g_ref, u1_ref, d2_ref, out_ref):
    lanes = 2 * out_ref.shape[3]
    pack(out_ref, 0, first_parts(x_ref, u1_ref, lanes), x_ref.shape[0])
    pack(out_ref, 7, last_parts(g_ref, d2_ref, lanes), x_ref.shape[0])


def activate(r_ref, u2_ref, slope_ref, hid_ref, tokens):
    hidden = u2_ref.shape[2]
    step = 256
    for j in range(2):
        mixed = unpack(r_ref, 0, j, tokens)
        for h in range(0, hidden, step):
            pre = tn(u2_ref[j, :, h : h + step], mixed)
            cumulative = 0.5 * (1.0 + lax.erf(pre * root_half))
            hid_ref[j, h : h + step] = (pre * cumulative).astype(bf16)
            density = jnp.exp(-0.5 * pre * pre) * norm_density
            slope_ref[j, h : h + step] = (cumulative + pre * density).astype(bf16)


def forward_kernel(r_ref, d1_ref, u2_ref, out_ref, slope_ref, hid_ref, *, tokens):
    activate(r_ref, u2_ref, slope_ref, hid_ref, tokens)
    pack(out_ref, 0, [tn(d1_ref[j], hid_ref[j]) for j in range(2)], tokens)


def top_kernel(
    r_ref, d1_ref, u2_ref, out_ref, slope_ref, hid_ref, mixed_ref, gd_ref, *, tokens
):
    activate(r_ref, u2_ref, slope_ref, hid_ref, tokens)
    mixed_ref[...] = r_ref[:, :7]
    gd_ref[...] = r_ref[:, 7:]
    backward(gd_ref, slope_ref, d1_ref, u2_ref, out_ref, tokens)


def backward(r_ref, slope_ref, d1_ref, u2_ref, out_ref, tokens):
    step = 256
    mixes = []
    for j in range(2):
        grad_down = unpack(r_ref, 0, j, tokens)
        grads = []
        for h in range(0, d1_ref.shape[1], step):
            grad_hidden = nn(d1_ref[j, h : h + step], grad_down)
            grads.append((grad_hidden * slope_ref[j, h : h + step]).astype(bf16))
        mixes.append(nn(u2_ref[j], jnp.concatenate(grads, axis=0)))
    pack(out_ref, 0, mixes, tokens)


def middle_kernel(r_ref, slope_ref, d1_ref, u2_ref, out_ref, *, tokens):
    backward(r_ref, slope_ref, d1_ref, u2_ref, out_ref, tokens)


def down_kernel(hid_ref, d1_ref, out_ref, *, tokens):
    pack(out_ref, 0, [tn(d1_ref[j], hid_ref[j]) for j in range(2)], tokens)


def head_kernel(g_ref, d2_ref, out_ref):
    pack(out_ref, 0, last_parts(g_ref, d2_ref, 2 * out_ref.shape[3]), g_ref.shape[0])


def tail_kernel(r_ref, g_ref, u1_ref, out_ref):
    tokens = g_ref.shape[0]
    width = u1_ref.shape[1]
    for i in range(2):
        cols = slice(i * width, (i + 1) * width)
        acts = nn(u1_ref[i], unpack(r_ref, 0, i, tokens)).T[:tokens]
        out_ref[:, cols] = (g_ref[:, cols].astype(f32) + acts).astype(bf16)


def main_terms_kernel(
    dp_ref, last_ref, g_ref, hid_ref, gd_ref, mixed_ref, slope_ref, d1_ref, *rest
):
    outs, low_ref = rest[:-1], rest[-1]
    tokens = g_ref.shape[0]
    hidden, lanes = hid_ref.shape[1:]
    width = g_ref.shape[1] // 2
    shares = len(outs)
    part, deep = width // shares, hidden // shares
    half = outs[0].shape[0] // 2

    def put(k, base, value):
        outs[k][base : base + value.shape[0]] = value.astype(bf16)

    def turned(n):
        spans = []
        for k in range(shares):
            d = lax.rem(dp_ref[0] + k, shares)
            spans.append(low_ref[n, pl.ds(pl.multiple_of(d * part, part), part)])
        return jnp.concatenate(spans, axis=0)

    for j in range(2):
        g = padded(g_ref[:, j * width : (j + 1) * width], lanes)
        grad_down = unpack(gd_ref, 0, j, tokens)
        low_ref[0] = unpack(last_ref, 0, j, tokens)
        low_ref[1] = unpack(mixed_ref, 0, j, tokens)
        start = j * half
        lows = nn(turned(0), g)
        for k in range(shares):
            put(k, start, lows[k * part : (k + 1) * part])
        for k in range(shares):
            d = lax.rem(dp_ref[0] + k, shares)
            rows = hid_ref[j, pl.ds(pl.multiple_of(d * deep, deep), deep)]
            put(k, start + part, nt(rows, grad_down))
        mixed = turned(1)
        for q in range(hidden // width):
            span = slice(q * width, (q + 1) * width)
            grad_hidden = nn(d1_ref[j, span], grad_down)
            grads = (grad_hidden * slope_ref[j, span]).astype(bf16)
            terms = nt(mixed, grads)
            for k in range(shares):
                put(k, start + part + deep + q * part, terms[k * part : (k + 1) * part])


def first_terms_kernel(dp_ref, x_ref, gf_ref, *rest):
    outs, xt_ref = rest[:-1], rest[-1]
    shares = len(outs)
    width, lanes = xt_ref.shape[1:]
    part = width // shares
    for i in range(2):
        grad_first = unpack(gf_ref, 0, i, x_ref.shape[0])
        rows = padded(x_ref[:, i * width : (i + 1) * width], lanes)
        xt_ref[i] = rows.astype(f32).T.astype(bf16)
        for k in range(shares):
            d = lax.rem(dp_ref[0] + k, shares)
            rows = xt_ref[i, pl.ds(pl.multiple_of(d * part, part), part)]
            outs[k][i * part : (i + 1) * part] = nt(rows, grad_first).astype(bf16)


def main_sum_kernel(*refs, factor):
    parts, (second_ref, down_ref, last_ref) = refs[:-3], refs[-3:]
    part, width = last_ref.shape[1:]
    deep = down_ref.shape[1]
    hidden = second_ref.shape[2]
    half = parts[0].shape[0] // 2

    def total(base, count):
        value = parts[0][base : base + count].astype(f32)
        for ref in parts[1:]:
            value = value + ref[base : base + count].astype(f32)
        return value * factor

    for j in range(2):
        start = j * half
        last_ref[j] = total(start, part)
        down_ref[j] = total(start + part, deep)
        for q in range(hidden // width):
            at = start + part + deep + q * part
            second_ref[j, :, q * width : (q + 1) * width] = total(at, part)


def first_sum_kernel(*refs, factor):
    parts, out_ref = refs[:-1], refs[-1]
    part = out_ref.shape[1]
    for i in range(2):
        value = parts[0][i * part : (i + 1) * part].astype(f32)
        for ref in parts[1:]:
            value = value + ref[i * part : (i + 1) * part].astype(f32)
        out_ref[i] = value * factor


def shuffle(value):
    return lax.all_to_all(value, "tensor", split_axis=0, concat_axis=0, tiled=True)


def spread(chunks):
    shares = len(chunks)
    moved = [chunks[0]]
    for k in range(1, shares):
        pairs = [(i, (i + k) % shares) for i in range(shares)]
        moved.append(lax.ppermute(chunks[k], "dp", pairs))
    return moved


def body(inputs, cotangent, up_first, up_second, down_first, down_second):
    x, u1, u2, d1, d2 = (inputs[0], up_first[0], up_second[0], down_first[0], down_second[0])
    tokens = x.shape[0]
    _, width, hidden = u2.shape
    peers = lax.axis_size("tensor")
    shares = lax.axis_size("dp")
    sections = lax.axis_size("pipe")
    section = lax.axis_index("pipe")
    dp_at = lax.axis_index("dp").astype(jnp.int32).reshape(1)
    factor = 1.0 / math.sqrt(tokens * shares)
    part, deep = width // shares, hidden // shares
    lanes = -(-tokens // 128) * 128
    packet = struct((peers, 7, 8, 128))
    rows = struct((tokens, 2 * width))
    tall = struct((2, hidden, lanes))
    block = 2 * 2 * width * lanes * width
    big = 2 * 2 * width * lanes * hidden

    def head(g):
        return call(head_kernel, [held(packet)], (g, d2), block)[0]

    def tail(r, g):
        return call(tail_kernel, [held(rows)], (r, g, u1), block)[0]

    def middle(gd):
        return call(
            functools.partial(middle_kernel, tokens=tokens), [held(packet)], (gd, slope, d1, u2), 2 * big
        )[0]

    def main_moved(last, g, gd):
        count = 2 * (part + deep + hidden * part // width)
        chunks = call(
            main_terms_kernel,
            [struct((count, width))] * shares,
            (dp_at, last, g, hid, gd, mixed, slope, d1),
            block + 3 * big,
            1,
            scratch=[pltpu.VMEM((2, width, lanes), bf16)],
        )
        return spread(chunks)

    def first_terms(gf):
        return call(
            first_terms_kernel,
            [struct((2 * part, width))] * shares,
            (dp_at, x, gf),
            block,
            1,
            scratch=[pltpu.VMEM((2, width, lanes), bf16)],
        )

    def main_sum(parts):
        return call(
            functools.partial(main_sum_kernel, factor=factor),
            [struct((2, part, hidden), f32), struct((2, deep, width), f32), struct((2, part, width), f32)],
            parts,
        )

    def first_sum(parts):
        return call(
            functools.partial(first_sum_kernel, factor=factor),
            [away(struct((2, part, width), f32))],
            parts,
        )[0]

    def finish(last, g, gd, gf, out):
        moved = main_moved(last, g, gd)
        first_moved = spread(first_terms(gf))
        second, down, low = main_sum(moved)
        return out, first_sum(first_moved), second, down, low

    def top():
        sent = call(
            top_entry_kernel,
            [held(struct((peers, 14, 8, 128)))],
            (far(x), far(cotangent), far(up_first[0]), far(down_second[0])),
            2 * block,
        )[0]
        sent, slope, hid, mixed, gd = call(
            functools.partial(top_kernel, tokens=tokens),
            [held(packet), tall, tall, packet, packet],
            (shuffle(sent), down_first[0], up_second[0]),
            3 * big,
        )
        gf = shuffle(sent)
        out = call(tail_kernel, [held(rows)], (gf, cotangent, up_first[0]), block)[0]
        return out, slope, hid, mixed, gf, gd

    def rest():
        sent = call(entry_kernel, [held(packet)], (far(x), far(up_first[0])), block)[0]
        mixed = shuffle(sent)
        sent, slope, hid = call(
            functools.partial(forward_kernel, tokens=tokens),
            [held(packet), tall, tall],
            (mixed, down_first[0], up_second[0]),
            2 * big,
        )
        last = lax.cond(section == 2, lambda: sent, lambda: shuffle(sent))
        return jnp.zeros(rows.shape, bf16), slope, hid, mixed, last, jnp.zeros(packet.shape, bf16)

    out3, slope, hid, mixed, r1, gd3 = lax.cond(section == sections - 1, top, rest)
    u1, d2, d1, u2 = call(
        stage_kernel, [held(u1), held(d2), held(d1), held(u2)], (u1, d2, d1, u2)
    )
    u1, d2, d1, u2 = near(u1), near(d2), near(d1), near(u2)

    def chain(g):
        gd = shuffle(head(g))
        gf = shuffle(middle(gd))
        return tail(gf, g), gd, gf

    def hand(value, source):
        return lax.ppermute(value, "pipe", [(source, source - 1)])

    g2 = hand(out3, 3)
    g2_near = near(g2)
    saved2 = lax.cond(section == 2, lambda: chain(g2_near), lambda: (out3, gd3, r1))
    g1 = hand(saved2[0], 2)
    g1_near = near(g1)
    saved = lax.cond(section == 1, lambda: chain(g1_near), lambda: saved2)
    g0 = near(hand(saved[0], 1))

    def last_turn():
        gd = shuffle(head(g0))
        sent = middle(gd)
        moved = main_moved(r1, g0, gd)
        gf = shuffle(sent)
        first_moved = spread(first_terms(gf))
        second, down, low = main_sum(moved)
        out = call(tail_kernel, [away(rows)], (gf, g0, u1), block)[0]
        first = first_sum(first_moved)
        return out, first, second, down, low

    def close(last):
        out, gd, gf = saved
        g = jnp.where(section == 3, cotangent, jnp.where(section == 2, g2, g1))
        return finish(last, g, gd, gf, call(stage_kernel, [away(rows)], (out,))[0])

    def close_late():
        sent = call(functools.partial(down_kernel, tokens=tokens), [packet], (hid, d1), big)[0]
        return close(shuffle(sent))

    branch = jnp.where(section == 0, 0, jnp.where(section == 1, 1, 2))
    done = lax.switch(branch, [last_turn, lambda: close(r1), close_late])
    out, first, second, down, low = done
    return (out[None], first[None], second[None], down[None], low[None])


def solution(mesh):
    return jax.shard_map(
        body,
        mesh=mesh,
        in_specs=(
            P("pipe", "dp", "tensor"),
            P("dp", "tensor"),
            P("pipe", "tensor", None, None),
            P("pipe", "tensor", None, None),
            P("pipe", "tensor", None, None),
            P("pipe", "tensor", None, None),
        ),
        out_specs=(
            P("pipe", "dp", "tensor"),
            P("pipe", "tensor", "dp", None),
            P("pipe", "tensor", "dp", None),
            P("pipe", "tensor", "dp", None),
            P("pipe", "tensor", "dp", None),
        ),
        check_vma=False,
    )
```
